32 devices in a mesh: tm: 4 (over z), band: 8 (over y, x, core).
Axes of the slice: x: 2, y: 2, z: 4, core: 2. Of those that a mesh axis runs over, the one named last changes fastest.
Arguments:
- tokens: bfloat16 [8, 32, 128, 768], P('tm', 'band'), may hold values from -6 to 6
- norm_gains: float32 [4, 768], replicated, may hold values from 0.25 to 1.75
- spatial_qkv: bfloat16 [768, 2304], replicated, may hold values from -4 to 4
- spatial_out: bfloat16 [768, 768], replicated, may hold values from -0.21875 to 0.21875
- temporal_qkv: bfloat16 [768, 2304], replicated, may hold values from -4 to 4
- temporal_out: bfloat16 [768, 768], replicated, may hold values from -0.21875 to 0.21875
- mlp_in: bfloat16 [768, 3072], replicated, may hold values from -0.21875 to 0.21875
- mlp_out: bfloat16 [3072, 768], replicated, may hold values from -0.109375 to 0.109375
Outputs:
- block_out: bfloat16 [8, 32, 128, 768], P('tm', 'band')
The draws below stay inside these ranges and needn't reach their ends.
All inputs are finite; a program needn't handle non-finite values.
Results may differ from the reference program's by a relative error of at most 0.035.
Values may be sent and summed in bfloat16 or wider, within the bound.
A program may use at most 128 MiB of HBM per device.

```python
import jax
import jax.numpy as jnp
from jax import lax

HEADS = 12
HEAD_DIM = 64
FF = 3072
POOL = 4
WID = 128
D = 768
FRAMES = 8
HGT = 32


def projection_table(key, table_seed):
    key = jax.random.fold_in(key, table_seed)
    key_query, key_keys, key_values = jax.random.split(key, 3)
    query_part = jnp.clip(jax.random.normal(key_query, (D, D), jnp.float32), -3.0, 3.0) * D ** (-0.5)
    key_part = jnp.clip(jax.random.normal(key_keys, (D, D), jnp.float32), -3.0, 3.0) * D ** (-0.5)
    value_part = jnp.clip(jax.random.normal(key_values, (D, D), jnp.float32), -3.0, 3.0) * D ** (-0.5)
    table = jnp.concatenate([query_part, key_part, value_part], axis=1)
    return jnp.clip(table, -4.0, 4.0).astype(jnp.bfloat16)


def draw_spatial_qkv(key, part):
    return projection_table(key, 11)


def draw_temporal_qkv(key, part):
    return projection_table(key, 12)


def draw_tokens(key, part):
    key = jax.random.fold_in(key, 13)
    key_base = jax.random.fold_in(key, 0)
    values = jnp.clip(jax.random.normal(key_base, (FRAMES, HGT, WID, D), jnp.float32), -6.0, 6.0)
    return values.astype(jnp.bfloat16)


def gaussian(key, dims, scale, reach, kind=jnp.bfloat16):
    values = jax.random.normal(key, dims, jnp.float32) * scale
    return jnp.minimum(jnp.maximum(values, -reach), reach).astype(kind)


def setup_inputs(seed: int = 0) -> dict:
    seeds = jax.random.split(jax.random.key(seed), 9)
    tokens = draw_tokens(jax.random.fold_in(seeds[8], 71), 0)
    norm_gains = jnp.clip(1.0 + 0.15 * jax.random.normal(seeds[1], (4, D), jnp.float32), 0.25, 1.75)
    spatial_qkv = draw_spatial_qkv(jax.random.fold_in(seeds[8], 71), 0)
    spatial_out = gaussian(seeds[3], (D, D), D ** -0.5, 0.21875)
    temporal_qkv = draw_temporal_qkv(jax.random.fold_in(seeds[8], 71), 0)
    temporal_out = gaussian(seeds[5], (D, D), D ** -0.5, 0.21875)
    mlp_in = gaussian(seeds[6], (D, FF), D ** -0.5, 0.21875)
    mlp_out = gaussian(seeds[7], (FF, D), FF ** -0.5, 0.109375)
    return {"tokens": tokens, "norm_gains": norm_gains, "spatial_qkv": spatial_qkv, "spatial_out": spatial_out, "temporal_qkv": temporal_qkv, "temporal_out": temporal_out, "mlp_in": mlp_in, "mlp_out": mlp_out}


def layer_normed(values, scaling):
    widened = values.astype(jnp.float32)
    average = lax.optimization_barrier(jnp.mean(widened, -1, keepdims=True))
    centred = widened - average
    spread = lax.optimization_barrier(jnp.mean(centred * centred, -1, keepdims=True))
    return centred * lax.rsqrt(spread + 1e-05) * scaling

def attend_heads(queries, paired):
    query_count = queries.shape[0]
    key_count = paired.shape[0]
    query_heads = queries.reshape(query_count, HEADS, HEAD_DIM).astype(jnp.float32)
    key_heads = paired[:, :D].reshape(key_count, HEADS, HEAD_DIM).astype(jnp.float32)
    value_heads = paired[:, D:].reshape(key_count, HEADS, HEAD_DIM).astype(jnp.float32)
    scores = jnp.einsum('qhd,khd->hqk', query_heads, key_heads) * HEAD_DIM ** (-0.5)
    weights = jax.nn.softmax(scores, axis=-1).astype(jnp.bfloat16)
    mixture = jnp.einsum('hqk,khd->qhd', weights.astype(jnp.float32), value_heads)
    return mixture.reshape(query_count, D).astype(jnp.bfloat16)

def reference(tokens, norm_gains, spatial_qkv, spatial_out, temporal_qkv, temporal_out, mlp_in, mlp_out):

    def spatial_frame(frame_tokens):
        normed = layer_normed(frame_tokens, norm_gains[0]).astype(jnp.bfloat16)
        pooled = lax.optimization_barrier(jnp.mean(normed.reshape(HGT // POOL, POOL, WID // POOL, POOL, D), axis=(1, 3), dtype=jnp.float32))
        keyed_rows = layer_normed(pooled, norm_gains[1]).astype(jnp.bfloat16).reshape(-1, D)
        queries = jnp.dot(normed.reshape(-1, D), spatial_qkv[:, :D], preferred_element_type=jnp.float32).astype(jnp.bfloat16)
        paired = jnp.dot(keyed_rows, spatial_qkv[:, D:], preferred_element_type=jnp.float32).astype(jnp.bfloat16)
        mixture = attend_heads(queries, paired)
        summed = frame_tokens.reshape(-1, D).astype(jnp.float32) + jnp.dot(mixture, spatial_out, preferred_element_type=jnp.float32)
        return summed.astype(jnp.bfloat16)
    first_sum = lax.map(spatial_frame, tokens)

    def project_frame(frame_rows):
        normed = layer_normed(frame_rows, norm_gains[2]).astype(jnp.bfloat16)
        return jnp.dot(normed, temporal_qkv, preferred_element_type=jnp.float32).astype(jnp.bfloat16)
    projected = lax.map(project_frame, first_sum)
    row_major = jnp.transpose(projected.reshape(FRAMES, HGT, WID, 3 * D), (1, 0, 2, 3))

    def temporal_row(row_block):
        frames_all = row_block.shape[0]
        position_count = row_block.shape[1]
        query_heads = row_block[..., :D].reshape(frames_all, position_count, HEADS, HEAD_DIM).astype(jnp.float32)
        key_heads = row_block[..., D:2 * D].reshape(frames_all, position_count, HEADS, HEAD_DIM).astype(jnp.float32)
        value_heads = row_block[..., 2 * D:].reshape(frames_all, position_count, HEADS, HEAD_DIM).astype(jnp.float32)
        scores = jnp.einsum('fphd,gphd->phfg', query_heads, key_heads) * HEAD_DIM ** (-0.5)
        weights = jax.nn.softmax(scores, axis=-1).astype(jnp.bfloat16)
        mixture = jnp.einsum('phfg,gphd->fphd', weights.astype(jnp.float32), value_heads)
        return mixture.reshape(frames_all, position_count, D).astype(jnp.bfloat16)
    temporal = lax.map(temporal_row, row_major)
    temporal = jnp.transpose(temporal, (1, 0, 2, 3)).reshape(FRAMES, HGT * WID, D)

    def finish_frame(operands):
        first_rows, temporal_rows = operands
        second_sum = (first_rows.astype(jnp.float32) + jnp.dot(temporal_rows, temporal_out, preferred_element_type=jnp.float32)).astype(jnp.bfloat16)
        third_normed = layer_normed(second_sum, norm_gains[3]).astype(jnp.bfloat16)
        hidden = jax.nn.gelu(jnp.dot(third_normed, mlp_in, preferred_element_type=jnp.float32), approximate=False).astype(jnp.bfloat16)
        return (second_sum.astype(jnp.float32) + jnp.dot(hidden, mlp_out, preferred_element_type=jnp.float32)).astype(jnp.bfloat16)
    result = lax.map(finish_frame, (first_sum, temporal))
    return result.reshape(FRAMES, HGT, WID, D)
```

```python
import functools

import jax
import jax.numpy as jnp
from jax import lax
from jax.experimental import pallas as pl
from jax.experimental.pallas import tpu as pltpu
from jax.sharding import PartitionSpec as P

HEAD_DIM = 64
POOL = 4
LANES = 128
GROUP = 16
MESH = pl.DeviceIdType.MESH
F32 = jnp.float32
BF16 = jnp.bfloat16


def layer_normed(values, scaling):
    widened = values.astype(F32)
    average = jnp.mean(widened, -1, keepdims=True)
    centred = widened - average
    spread = jnp.mean(centred * centred, -1, keepdims=True)
    return centred * lax.rsqrt(spread + 1e-05) * scaling


def dot(a, b):
    return jnp.dot(a, b, preferred_element_type=F32)


def dot_t(a, b):
    return lax.dot_general(a, b, (((1,), (1,)), ((), ())), preferred_element_type=F32)


def ones_split(rows):
    lane = lax.broadcasted_iota(jnp.int32, (rows, LANES), 1)
    first = jnp.where(lane < HEAD_DIM, 1.0, 0.0).astype(BF16)
    second = jnp.where(lane < HEAD_DIM, 0.0, 1.0).astype(BF16)
    return first, second


def block_kernel(
    n, nb, cols, part,
    tokens_ref, gains_ref, wsq_ref, wso_ref, wtq_ref, wto_ref, w1_ref, w2_ref,
    out_ref,
    x, sq, so, tq, to, m1, m2, normed, keyed, kst, vst, fs, send1, recv1, send2, recv2, proj,
    load_sem, band_send, band_recv, s1_send, s1_recv, s2_send, s2_recv,
):
    frames, tokens_here, d = x.shape
    steps = fs.shape[0]
    share = tokens_here // n
    keys = keyed.shape[2]
    all_keys = nb * keys
    slabs = d // LANES
    chunk = frames * n * part
    me = lax.axis_index("tm")
    band = lax.axis_index("band")

    loads = [
        pltpu.make_async_copy(src, dst, load_sem.at[i])
        for i, (src, dst) in enumerate(
            ((tokens_ref, x), (wsq_ref, sq), (wso_ref, so), (wtq_ref, tq), (wto_ref, to), (w1_ref, m1), (w2_ref, m2))
        )
    ]
    for load in loads:
        load.start()

    barrier = pltpu.get_barrier_semaphore()
    for step in range(1, n):
        pl.semaphore_signal(barrier, inc=1, device_id={"tm": lax.rem(me + step, n)}, device_id_type=MESH)
    for step in range(1, nb):
        pl.semaphore_signal(barrier, inc=1, device_id={"band": lax.rem(band + step, nb)}, device_id_type=MESH)

    gain = [gains_ref[i : i + 1, :] for i in range(4)]
    loads[0].wait()
    for f in range(frames):
        @pl.loop(0, tokens_here // LANES)
        def _(i):
            rows = pl.ds(pl.multiple_of(i * LANES, LANES), LANES)
            normed[f, rows, :] = layer_normed(x[f, rows, :], gain[0]).astype(BF16)

    place = lax.broadcasted_iota(jnp.int32, (keys, tokens_here), 1)
    want = lax.broadcasted_iota(jnp.int32, (keys, tokens_here), 0)
    cell = (place // (cols * POOL)) * (cols // POOL) + (place % cols) // POOL
    pool = jnp.where(cell == want, 1.0 / (POOL * POOL), 0.0).astype(BF16)
    for f in range(frames):
        pooled = dot(pool, normed[f])
        keyed[band, f] = layer_normed(pooled, gain[1]).astype(BF16)

    pl.semaphore_wait(barrier, n + nb - 2)

    def band_copy(step, slot):
        return pltpu.make_async_remote_copy(
            src_ref=keyed.at[slot], dst_ref=keyed.at[slot],
            send_sem=band_send.at[step], recv_sem=band_recv.at[step],
            device_id={"band": lax.rem(band + step, nb)}, device_id_type=MESH,
        )

    for step in range(1, nb):
        band_copy(step, band).start()
    loads[1].wait()
    loads[2].wait()
    for step in range(1, nb):
        band_copy(step, lax.rem(band + nb - step, nb)).wait_recv()

    first_ones, second_ones = ones_split(all_keys)
    high = lax.broadcasted_iota(jnp.int32, (LANES, all_keys), 0) >= HEAD_DIM
    right = lax.broadcasted_iota(jnp.int32, (all_keys, LANES), 1) >= HEAD_DIM

    for f in range(frames):
        @pl.loop(0, slabs)
        def _(h):
            rows = jnp.concatenate([keyed[b, f] for b in range(nb)], axis=0)
            lanes = pl.ds(pl.multiple_of(d + h * LANES, LANES), LANES)
            k = dot(rows, sq[:, lanes]).T
            kst[f, h] = jnp.concatenate(
                [jnp.where(high, 0.0, k).astype(BF16), jnp.where(high, k, 0.0).astype(BF16)], axis=1
            )
            lanes = pl.ds(pl.multiple_of(2 * d + h * LANES, LANES), LANES)
            v = dot(rows, sq[:, lanes])
            vst[f, h, :all_keys, :] = jnp.concatenate([jnp.where(right, 0.0, v).astype(BF16), first_ones], axis=1)
            vst[f, h, all_keys:, :] = jnp.concatenate([jnp.where(right, v, 0.0).astype(BF16), second_ones], axis=1)

    def out_copy(j, step, slot):
        return pltpu.make_async_remote_copy(
            src_ref=send1.at[j, :, lax.rem(me + step, n)], dst_ref=recv1.at[j, :, slot],
            send_sem=s1_send.at[j, step], recv_sem=s1_recv.at[j, step],
            device_id={"tm": lax.rem(me + step, n)}, device_id_type=MESH,
        )

    def back_copy(j, step, slot):
        return pltpu.make_async_remote_copy(
            src_ref=send2.at[j, :, lax.rem(me + step, n)], dst_ref=recv2.at[j, :, slot],
            send_sem=s2_send.at[j, step], recv_sem=s2_recv.at[j, step],
            device_id={"tm": lax.rem(me + step, n)}, device_id_type=MESH,
        )

    def rows_of(j, r):
        return pl.ds(pl.multiple_of(r * share + j * part, part), part)

    def spatial(j, carry):
        base = jnp.concatenate(
            [normed[f, rows_of(j, r), :] for f in range(frames) for r in range(n)], axis=0
        )
        q = (dot(base, sq[:, :d]) * HEAD_DIM ** (-0.5)).astype(BF16)
        mixed = []
        for f in range(frames):
            heads = []
            for h in range(slabs):
                qh = q[f * n * part : (f + 1) * n * part, h * LANES : (h + 1) * LANES]
                s = dot(qh, kst[f, h])
                a, b = s[:, :all_keys], s[:, all_keys:]
                a = jnp.exp(a - jnp.max(a, -1, keepdims=True)).astype(BF16)
                b = jnp.exp(b - jnp.max(b, -1, keepdims=True)).astype(BF16)
                o = dot(jnp.concatenate([a, b], axis=1), vst[f, h])
                heads.append((o[:, :LANES] / o[:, LANES:]).astype(BF16))
            mixed.append(jnp.concatenate(heads, axis=1))
        summed = dot(jnp.concatenate(mixed, axis=0), so[...])
        own = jnp.concatenate([x[f, rows_of(j, r), :] for f in range(frames) for r in range(n)], axis=0)
        first = (own.astype(F32) + summed).astype(BF16)
        fs[j] = first.reshape(frames, n, part, d)
        send1[j] = layer_normed(first, gain[2]).astype(BF16).reshape(frames, n, part, d)
        recv1[j, :, me] = send1[j, :, me]
        for step in range(1, n):
            out_copy(j, step, me).start()
        return carry

    lax.fori_loop(0, steps, spatial, 0)
    loads[3].wait()

    cells = frames * n * GROUP
    g_first, g_second = ones_split(cells)
    g_right = lax.broadcasted_iota(jnp.int32, (cells, LANES), 1) >= HEAD_DIM
    row_at = lax.broadcasted_iota(jnp.int32, (cells, cells), 0) % GROUP
    col_at = lax.broadcasted_iota(jnp.int32, (cells, cells), 1) % GROUP
    bias = jnp.where(row_at == col_at, 0.0, -1e30).astype(F32)

    def temporal(j, carry):
        for step in range(1, n):
            out_copy(j, step, lax.rem(me + n - step, n)).wait_recv()
        base = recv1[j].reshape(chunk, d)
        for c in range(3):
            part_proj = dot(base, tq[:, c * d : (c + 1) * d])
            if c == 0:
                part_proj = part_proj * HEAD_DIM ** (-0.5)
            proj[:, :, c * d : (c + 1) * d] = part_proj.astype(BF16).reshape(frames * n, part, d)
        zero = jnp.zeros((cells, LANES), BF16)
        for g in range(part // GROUP):
            at = slice(g * GROUP, (g + 1) * GROUP)
            heads = []
            for h in range(slabs):
                q, k, v = (
                    proj[:, at, c * d + h * LANES : c * d + (h + 1) * LANES].reshape(cells, LANES) for c in range(3)
                )
                kk = jnp.concatenate([jnp.where(g_right, zero, k), jnp.where(g_right, k, zero)], axis=0)
                vv = jnp.concatenate(
                    [
                        jnp.concatenate([jnp.where(g_right, zero, v), g_first], axis=1),
                        jnp.concatenate([jnp.where(g_right, v, zero), g_second], axis=1),
                    ],
                    axis=0,
                )
                s = dot_t(q, kk)
                a, b = s[:, :cells] + bias, s[:, cells:] + bias
                a = jnp.exp(a - jnp.max(a, -1, keepdims=True)).astype(BF16)
                b = jnp.exp(b - jnp.max(b, -1, keepdims=True)).astype(BF16)
                o = dot(jnp.concatenate([a, b], axis=1), vv)
                heads.append((o[:, :LANES] / o[:, LANES:]).astype(BF16))
            send2[j, :, :, at, :] = jnp.concatenate(heads, axis=1).reshape(frames, n, GROUP, d)
        recv2[j, :, me] = send2[j, :, me]
        for step in range(1, n):
            back_copy(j, step, me).start()
        return carry

    lax.fori_loop(0, steps, temporal, 0)
    for load in loads[4:]:
        load.wait()

    hidden_part = d

    def finish(j, carry):
        for step in range(1, n):
            back_copy(j, step, lax.rem(me + n - step, n)).wait_recv()
        mix = recv2[j].reshape(chunk, d)
        second = (fs[j].reshape(chunk, d).astype(F32) + dot(mix, to[...])).astype(BF16)
        third = layer_normed(second, gain[3]).astype(BF16)
        total = second.astype(F32)
        for c in range(m1.shape[1] // hidden_part):
            span = slice(c * hidden_part, (c + 1) * hidden_part)
            u = dot(third, m1[:, span])
            u = (0.5 * u * (1.0 + lax.erf(u * 0.5**0.5))).astype(BF16)
            total = total + dot(u, m2[span, :])
        total = total.astype(BF16)
        for f in range(frames):
            for r in range(n):
                start = (f * n + r) * part
                out_ref[f, rows_of(j, r), :] = total[start : start + part]
        return carry

    lax.fori_loop(0, steps, finish, 0)

    for step in range(1, nb):
        band_copy(step, band).wait_send()

    def drain(j, carry):
        for step in range(1, n):
            out_copy(j, step, me).wait_send()
            back_copy(j, step, me).wait_send()
        return carry

    lax.fori_loop(0, steps, drain, 0)


def local(n, nb, tokens, norm_gains, spatial_qkv, spatial_out, temporal_qkv, temporal_out, mlp_in, mlp_out):
    frames, rows, cols, d = tokens.shape
    tokens_here = rows * cols
    keys = tokens_here // (POOL * POOL)
    share = tokens_here // n
    part = min(2 * GROUP, share)
    steps = share // part
    slabs = d // LANES
    all_keys = nb * keys
    any_spec = pl.BlockSpec(memory_space=pl.ANY)
    vmem_spec = pl.BlockSpec(memory_space=pltpu.VMEM)
    moved = pltpu.VMEM((steps, frames, n, part, d), BF16)
    dma = pltpu.SemaphoreType.DMA
    result = pl.pallas_call(
        functools.partial(block_kernel, n, nb, cols, part),
        out_shape=jax.ShapeDtypeStruct((frames, tokens_here, d), BF16),
        in_specs=[any_spec, vmem_spec] + [any_spec] * 6,
        out_specs=vmem_spec,
        scratch_shapes=[
            pltpu.VMEM((frames, tokens_here, d), BF16),
            pltpu.VMEM(spatial_qkv.shape, BF16),
            pltpu.VMEM(spatial_out.shape, BF16),
            pltpu.VMEM(temporal_qkv.shape, BF16),
            pltpu.VMEM(temporal_out.shape, BF16),
            pltpu.VMEM(mlp_in.shape, BF16),
            pltpu.VMEM(mlp_out.shape, BF16),
            pltpu.VMEM((frames, tokens_here, d), BF16),
            pltpu.VMEM((nb, frames, keys, d), BF16),
            pltpu.VMEM((frames, slabs, LANES, 2 * all_keys), BF16),
            pltpu.VMEM((frames, slabs, 2 * all_keys, 2 * LANES), BF16),
            moved, moved, moved, moved, moved,
            pltpu.VMEM((frames * n, part, 3 * d), BF16),
            dma((7,)),
            dma((nb,)), dma((nb,)),
            dma((steps, n)), dma((steps, n)), dma((steps, n)), dma((steps, n)),
        ],
        compiler_params=pltpu.CompilerParams(
            collective_id=0, has_side_effects=True, vmem_limit_bytes=60 * 1024 * 1024
        ),
        name="block",
    )(
        tokens.reshape(frames, tokens_here, d), norm_gains, spatial_qkv, spatial_out,
        temporal_qkv, temporal_out, mlp_in, mlp_out,
    )
    return result.reshape(tokens.shape)


def solution(mesh):
    n, nb = mesh.shape["tm"], mesh.shape["band"]
    in_specs = (P("tm", "band", None, None), P(), P(), P(), P(), P(), P(), P())
    out_specs = P("tm", "band", None, None)
    return jax.shard_map(
        functools.partial(local, n, nb), mesh=mesh, in_specs=in_specs, out_specs=out_specs, check_vma=False
    )
```

```python
import functools

import jax
import jax.numpy as jnp
from jax import lax
from jax.experimental import pallas as pl
from jax.experimental.pallas import tpu as pltpu
from jax.sharding import PartitionSpec as P

HEAD_DIM = 64
POOL = 4
LANES = 128
GROUP = 16
MESH = pl.DeviceIdType.MESH
F32 = jnp.float32
BF16 = jnp.bfloat16


def layer_normed(values, scaling):
    widened = values.astype(F32)
    average = jnp.mean(widened, -1, keepdims=True)
    centred = widened - average
    spread = jnp.mean(centred * centred, -1, keepdims=True)
    return centred * lax.rsqrt(spread + 1e-05) * scaling


def dot(a, b):
    return jnp.dot(a, b, preferred_element_type=F32)


def dot_t(a, b):
    return lax.dot_general(a, b, (((1,), (1,)), ((), ())), preferred_element_type=F32)


def ones_split(rows):
    lane = lax.broadcasted_iota(jnp.int32, (rows, LANES), 1)
    first = jnp.where(lane < HEAD_DIM, 1.0, 0.0).astype(BF16)
    second = jnp.where(lane < HEAD_DIM, 0.0, 1.0).astype(BF16)
    return first, second


def block_kernel(
    n, nb, cols, part,
    tokens_ref, gains_ref, wsq_ref, wso_ref, wtq_ref, wto_ref, w1_ref, w2_ref,
    out_ref,
    x, sq, so, tq, to, m1, m2, normed, queries, keyed, kst, vst, fs, send1, recv1, send2, recv2, proj,
    x_sem, load_sem, leave_sem, even_send, even_recv, pair_send, pair_recv, s1_send, s1_recv, s2_send, s2_recv,
):
    frames, tokens_here, d = x.shape
    steps = fs.shape[0]
    share = tokens_here // n
    keys = keyed.shape[2]
    all_keys = nb * keys
    slabs = d // LANES
    chunk = frames * n * part
    me = lax.axis_index("tm")
    band = lax.axis_index("band")

    loads = [
        pltpu.make_async_copy(src, dst, load_sem.at[i])
        for i, (src, dst) in enumerate(
            ((wsq_ref, sq), (wso_ref, so), (wtq_ref, tq), (wto_ref, to), (w1_ref, m1), (w2_ref, m2))
        )
    ]
    arrive = [pltpu.make_async_copy(tokens_ref.at[f], x.at[f], x_sem.at[f]) for f in range(frames)]
    for load in arrive:
        load.start()

    pairs = nb // 2
    partner = band + 1 - 2 * lax.rem(band, 2)
    order = sorted(range(1, n), key=lambda step: abs(2 * step - n))
    barrier = pltpu.get_barrier_semaphore()
    for step in order:
        pl.semaphore_signal(barrier, inc=1, device_id={"tm": lax.rem(me + step, n)}, device_id_type=MESH)
    for step in range(1, pairs):
        pl.semaphore_signal(barrier, inc=1, device_id={"band": lax.rem(band + 2 * step, nb)}, device_id_type=MESH)
    pl.semaphore_signal(barrier, inc=1, device_id={"band": partner}, device_id_type=MESH)

    def even_copy(f, step, slot):
        return pltpu.make_async_remote_copy(
            src_ref=keyed.at[f, slot], dst_ref=keyed.at[f, slot],
            send_sem=even_send.at[f, step], recv_sem=even_recv.at[f, step],
            device_id={"band": lax.rem(band + 2 * step, nb)}, device_id_type=MESH,
        )

    def pair_copy(f, step, slot):
        return pltpu.make_async_remote_copy(
            src_ref=keyed.at[f, slot], dst_ref=keyed.at[f, slot],
            send_sem=pair_send.at[f, step], recv_sem=pair_recv.at[f, step],
            device_id={"band": partner}, device_id_type=MESH,
        )

    def behind(index, step):
        return lax.rem(index + nb - 2 * step, nb)

    gain = [gains_ref[i : i + 1, :] for i in range(4)]
    place = lax.broadcasted_iota(jnp.int32, (keys, tokens_here), 1)
    want = lax.broadcasted_iota(jnp.int32, (keys, tokens_here), 0)
    cell = (place // (cols * POOL)) * (cols // POOL) + (place % cols) // POOL
    pool = jnp.where(cell == want, 1.0 / (POOL * POOL), 0.0).astype(BF16)
    for f in range(frames):
        arrive[f].wait()
        if f == 0:
            loads[0].start()

        @pl.loop(0, tokens_here // LANES)
        def _(i):
            rows = pl.ds(pl.multiple_of(i * LANES, LANES), LANES)
            normed[f, rows, :] = layer_normed(x[f, rows, :], gain[0]).astype(BF16)

        keyed[f, band] = layer_normed(dot(pool, normed[f]), gain[1]).astype(BF16)
        if f == 0:
            pl.semaphore_wait(barrier, n - 1 + pairs)
        for step in range(1, pairs):
            even_copy(f, step, band).start()
        pair_copy(f, 0, band).start()
    for load in loads[1:]:
        load.start()
    loads[0].wait()

    wide = 2 * LANES
    for f in range(frames):
        @pl.loop(0, tokens_here // wide)
        def _(i):
            rows = pl.ds(pl.multiple_of(i * wide, wide), wide)
            queries[f, rows, :] = (dot(normed[f, rows, :], sq[:, :d]) * HEAD_DIM ** (-0.5)).astype(BF16)

        for step in range(1, pairs):
            even_copy(f, step, behind(band, step)).wait_recv()
            pair_copy(f, step, behind(band, step)).start()

    first_ones, second_ones = ones_split(all_keys)
    high = lax.broadcasted_iota(jnp.int32, (LANES, all_keys), 0) >= HEAD_DIM
    right = lax.broadcasted_iota(jnp.int32, (all_keys, LANES), 1) >= HEAD_DIM

    for f in range(frames):
        for step in range(pairs):
            pair_copy(f, step, behind(partner, step)).wait_recv()
        rows = keyed[f].reshape(all_keys, d)
        for h in range(0, slabs, 2):
            both_k = dot(rows, sq[:, d + h * LANES : d + (h + 2) * LANES])
            both_v = dot(rows, sq[:, 2 * d + h * LANES : 2 * d + (h + 2) * LANES])
            for i in range(2):
                k = both_k[:, i * LANES : (i + 1) * LANES].T
                v = both_v[:, i * LANES : (i + 1) * LANES]
                kst[f, h + i] = jnp.concatenate(
                    [jnp.where(high, 0.0, k).astype(BF16), jnp.where(high, k, 0.0).astype(BF16)], axis=1
                )
                vst[f, h + i, :all_keys, :] = jnp.concatenate(
                    [jnp.where(right, 0.0, v).astype(BF16), first_ones], axis=1
                )
                vst[f, h + i, all_keys:, :] = jnp.concatenate(
                    [jnp.where(right, v, 0.0).astype(BF16), second_ones], axis=1
                )
    loads[1].wait()

    def out_copy(j, step, slot):
        return pltpu.make_async_remote_copy(
            src_ref=send1.at[j, :, lax.rem(me + step, n)], dst_ref=recv1.at[j, :, slot],
            send_sem=s1_send.at[j, step], recv_sem=s1_recv.at[j, step],
            device_id={"tm": lax.rem(me + step, n)}, device_id_type=MESH,
        )

    def back_copy(j, step, slot):
        return pltpu.make_async_remote_copy(
            src_ref=send2.at[j, :, lax.rem(me + step, n)], dst_ref=recv2.at[j, :, slot],
            send_sem=s2_send.at[j, step], recv_sem=s2_recv.at[j, step],
            device_id={"tm": lax.rem(me + step, n)}, device_id_type=MESH,
        )

    def rows_of(j, r):
        return pl.ds(pl.multiple_of(r * share + j * part, part), part)

    def spatial(j, carry):
        mixed = []
        for f in range(frames):
            q = jnp.concatenate([queries[f, rows_of(j, r), :] for r in range(n)], axis=0)
            heads = []
            for h in range(slabs):
                qh = q[:, h * LANES : (h + 1) * LANES]
                s = dot(qh, kst[f, h])
                a, b = s[:, :all_keys], s[:, all_keys:]
                a = jnp.exp(a - jnp.max(a, -1, keepdims=True)).astype(BF16)
                b = jnp.exp(b - jnp.max(b, -1, keepdims=True)).astype(BF16)
                o = dot(jnp.concatenate([a, b], axis=1), vst[f, h])
                heads.append((o[:, :LANES] / o[:, LANES:]).astype(BF16))
            mixed.append(jnp.concatenate(heads, axis=1))
        summed = dot(jnp.concatenate(mixed, axis=0), so[...])
        own = jnp.concatenate([x[f, rows_of(j, r), :] for f in range(frames) for r in range(n)], axis=0)
        first = (own.astype(F32) + summed).astype(BF16)
        fs[j] = first.reshape(frames, n, part, d)
        send1[j] = layer_normed(first, gain[2]).astype(BF16).reshape(frames, n, part, d)
        recv1[j, :, me] = send1[j, :, me]
        for step in order:
            out_copy(j, step, me).start()
        return carry

    lax.fori_loop(0, steps, spatial, 0)
    loads[2].wait()

    cells = frames * n * GROUP
    g_first, g_second = ones_split(cells)
    g_right = lax.broadcasted_iota(jnp.int32, (cells, LANES), 1) >= HEAD_DIM
    row_at = lax.broadcasted_iota(jnp.int32, (cells, cells), 0) % GROUP
    col_at = lax.broadcasted_iota(jnp.int32, (cells, cells), 1) % GROUP
    bias = jnp.where(row_at == col_at, 0.0, -1e30).astype(F32)

    def temporal(j, carry):
        for step in range(1, n):
            out_copy(j, step, lax.rem(me + n - step, n)).wait_recv()
        base = recv1[j].reshape(chunk, d)
        for c in range(3):
            part_proj = dot(base, tq[:, c * d : (c + 1) * d])
            if c == 0:
                part_proj = part_proj * HEAD_DIM ** (-0.5)
            proj[:, :, c * d : (c + 1) * d] = part_proj.astype(BF16).reshape(frames * n, part, d)
        zero = jnp.zeros((cells, LANES), BF16)
        for g in range(part // GROUP):
            at = slice(g * GROUP, (g + 1) * GROUP)
            heads = []
            for h in range(slabs):
                q, k, v = (
                    proj[:, at, c * d + h * LANES : c * d + (h + 1) * LANES].reshape(cells, LANES) for c in range(3)
                )
                kk = jnp.concatenate([jnp.where(g_right, zero, k), jnp.where(g_right, k, zero)], axis=0)
                vv = jnp.concatenate(
                    [
                        jnp.concatenate([jnp.where(g_right, zero, v), g_first], axis=1),
                        jnp.concatenate([jnp.where(g_right, v, zero), g_second], axis=1),
                    ],
                    axis=0,
                )
                s = dot_t(q, kk)
                a, b = s[:, :cells] + bias, s[:, cells:] + bias
                a = jnp.exp(a - jnp.max(a, -1, keepdims=True)).astype(BF16)
                b = jnp.exp(b - jnp.max(b, -1, keepdims=True)).astype(BF16)
                o = dot(jnp.concatenate([a, b], axis=1), vv)
                heads.append((o[:, :LANES] / o[:, LANES:]).astype(BF16))
            send2[j, :, :, at, :] = jnp.concatenate(heads, axis=1).reshape(frames, n, GROUP, d)
        recv2[j, :, me] = send2[j, :, me]
        for step in order:
            back_copy(j, step, me).start()
        return carry

    lax.fori_loop(0, steps, temporal, 0)
    for load in loads[3:]:
        load.wait()

    hidden_part = d

    def leave(j):
        rows = pl.ds(pl.multiple_of(j * part, part), part)
        return pltpu.make_async_copy(send1.at[j], out_ref.at[:, :, rows, :], leave_sem.at[j])

    def finish(j, carry):
        for step in range(1, n):
            out_copy(j, step, me).wait_send()
        for step in range(1, n):
            back_copy(j, step, lax.rem(me + n - step, n)).wait_recv()
        mix = recv2[j].reshape(chunk, d)
        second = (fs[j].reshape(chunk, d).astype(F32) + dot(mix, to[...])).astype(BF16)
        third = layer_normed(second, gain[3]).astype(BF16)
        total = second.astype(F32)
        for c in range(m1.shape[1] // hidden_part):
            span = slice(c * hidden_part, (c + 1) * hidden_part)
            u = dot(third, m1[:, span])
            u = (0.5 * u * (1.0 + lax.erf(u * 0.5**0.5))).astype(BF16)
            total = total + dot(u, m2[span, :])
        send1[j] = total.astype(BF16).reshape(frames, n, part, d)
        leave(j).start()
        return carry

    lax.fori_loop(0, steps, finish, 0)

    for f in range(frames):
        for step in range(1, pairs):
            even_copy(f, step, band).wait_send()
        for step in range(pairs):
            pair_copy(f, step, behind(band, step)).wait_send()

    def drain(j, carry):
        for step in range(1, n):
            back_copy(j, step, me).wait_send()
        leave(j).wait()
        return carry

    lax.fori_loop(0, steps, drain, 0)


def local(n, nb, tokens, norm_gains, spatial_qkv, spatial_out, temporal_qkv, temporal_out, mlp_in, mlp_out):
    frames, rows, cols, d = tokens.shape
    tokens_here = rows * cols
    keys = tokens_here // (POOL * POOL)
    share = tokens_here // n
    part = min(2 * GROUP, share)
    steps = share // part
    slabs = d // LANES
    all_keys = nb * keys
    any_spec = pl.BlockSpec(memory_space=pl.ANY)
    vmem_spec = pl.BlockSpec(memory_space=pltpu.VMEM)
    moved = pltpu.VMEM((steps, frames, n, part, d), BF16)
    dma = pltpu.SemaphoreType.DMA
    result = pl.pallas_call(
        functools.partial(block_kernel, n, nb, cols, part),
        out_shape=jax.ShapeDtypeStruct((frames, n, share, d), BF16),
        in_specs=[any_spec, vmem_spec] + [any_spec] * 6,
        out_specs=any_spec,
        scratch_shapes=[
            pltpu.VMEM((frames, tokens_here, d), BF16),
            pltpu.VMEM(spatial_qkv.shape, BF16),
            pltpu.VMEM(spatial_out.shape, BF16),
            pltpu.VMEM(temporal_qkv.shape, BF16),
            pltpu.VMEM(temporal_out.shape, BF16),
            pltpu.VMEM(mlp_in.shape, BF16),
            pltpu.VMEM(mlp_out.shape, BF16),
            pltpu.VMEM((frames, tokens_here, d), BF16),
            pltpu.VMEM((frames, tokens_here, d), BF16),
            pltpu.VMEM((frames, nb, keys, d), BF16),
            pltpu.VMEM((frames, slabs, LANES, 2 * all_keys), BF16),
            pltpu.VMEM((frames, slabs, 2 * all_keys, 2 * LANES), BF16),
            moved, moved, moved, moved, moved,
            pltpu.VMEM((frames * n, part, 3 * d), BF16),
            dma((frames,)), dma((6,)), dma((steps,)),
            dma((frames, nb // 2)), dma((frames, nb // 2)), dma((frames, nb // 2)), dma((frames, nb // 2)),
            dma((steps, n)), dma((steps, n)), dma((steps, n)), dma((steps, n)),
        ],
        compiler_params=pltpu.CompilerParams(
            collective_id=0, has_side_effects=True, vmem_limit_bytes=60 * 1024 * 1024
        ),
        name="block",
    )(
        tokens.reshape(frames, tokens_here, d), norm_gains, spatial_qkv, spatial_out,
        temporal_qkv, temporal_out, mlp_in, mlp_out,
    )
    return result.reshape(tokens.shape)


def solution(mesh):
    n, nb = mesh.shape["tm"], mesh.shape["band"]
    in_specs = (P("tm", "band", None, None), P(), P(), P(), P(), P(), P(), P())
    out_specs = P("tm", "band", None, None)
    return jax.shard_map(
        functools.partial(local, n, nb), mesh=mesh, in_specs=in_specs, out_specs=out_specs, check_vma=False
    )
```

```python
import functools

import jax
import jax.numpy as jnp
from jax import lax
from jax.experimental import pallas as pl
from jax.experimental.pallas import tpu as pltpu
from jax.sharding import PartitionSpec as P

HEAD_DIM = 64
POOL = 4
LANES = 128
GROUP = 16
MESH = pl.DeviceIdType.MESH
F32 = jnp.float32
BF16 = jnp.bfloat16


def layer_normed(values, scaling):
    widened = values.astype(F32)
    average = jnp.mean(widened, -1, keepdims=True)
    centred = widened - average
    spread = jnp.mean(centred * centred, -1, keepdims=True)
    return centred * lax.rsqrt(spread + 1e-05) * scaling


def dot(a, b):
    return jnp.dot(a, b, preferred_element_type=F32)


def dot_t(a, b):
    return lax.dot_general(a, b, (((1,), (1,)), ((), ())), preferred_element_type=F32)


def ones_split(rows):
    lane = lax.broadcasted_iota(jnp.int32, (rows, LANES), 1)
    first = jnp.where(lane < HEAD_DIM, 1.0, 0.0).astype(BF16)
    second = jnp.where(lane < HEAD_DIM, 0.0, 1.0).astype(BF16)
    return first, second


def block_kernel(
    n, nb, cols, part,
    tokens_ref, gains_ref, wsq_ref, wso_ref, wtq_ref, wto_ref, w1_ref, w2_ref,
    out_ref,
    x, sq, so, tq, to, m1, m2, normed, queries, keyed, kst, vst, fs, send1, recv1, send2, recv2, proj,
    x_sem, load_sem, even_send, even_recv, pair_send, pair_recv, s1_send, s1_recv, s2_send, s2_recv,
):
    frames, tokens_here, d = x.shape
    steps = fs.shape[0]
    share = tokens_here // n
    keys = keyed.shape[2]
    all_keys = nb * keys
    slabs = d // LANES
    chunk = frames * n * part
    me = lax.axis_index("tm")
    band = lax.axis_index("band")

    loads = [
        pltpu.make_async_copy(src, dst, load_sem.at[i])
        for i, (src, dst) in enumerate(
            ((wsq_ref, sq), (wso_ref, so), (wtq_ref, tq), (wto_ref, to), (w1_ref, m1), (w2_ref, m2))
        )
    ]
    arrive = [pltpu.make_async_copy(tokens_ref.at[f], x.at[f], x_sem.at[f]) for f in range(frames)]
    for load in arrive:
        load.start()

    pairs = nb // 2
    partner = band + 1 - 2 * lax.rem(band, 2)
    order = sorted(range(1, n), key=lambda step: abs(2 * step - n))
    barrier = pltpu.get_barrier_semaphore()
    for step in order:
        pl.semaphore_signal(barrier, inc=1, device_id={"tm": lax.rem(me + step, n)}, device_id_type=MESH)
    for step in range(1, pairs):
        pl.semaphore_signal(barrier, inc=1, device_id={"band": lax.rem(band + 2 * step, nb)}, device_id_type=MESH)
    pl.semaphore_signal(barrier, inc=1, device_id={"band": partner}, device_id_type=MESH)

    def even_copy(f, step, slot):
        return pltpu.make_async_remote_copy(
            src_ref=keyed.at[f, slot], dst_ref=keyed.at[f, slot],
            send_sem=even_send.at[f, step], recv_sem=even_recv.at[f, step],
            device_id={"band": lax.rem(band + 2 * step, nb)}, device_id_type=MESH,
        )

    def pair_copy(f, step, slot):
        return pltpu.make_async_remote_copy(
            src_ref=keyed.at[f, slot], dst_ref=keyed.at[f, slot],
            send_sem=pair_send.at[f, step], recv_sem=pair_recv.at[f, step],
            device_id={"band": partner}, device_id_type=MESH,
        )

    def behind(index, step):
        return lax.rem(index + nb - 2 * step, nb)

    gain = [gains_ref[i : i + 1, :] for i in range(4)]
    place = lax.broadcasted_iota(jnp.int32, (keys, tokens_here), 1)
    want = lax.broadcasted_iota(jnp.int32, (keys, tokens_here), 0)
    cell = (place // (cols * POOL)) * (cols // POOL) + (place % cols) // POOL
    pool = jnp.where(cell == want, 1.0 / (POOL * POOL), 0.0).astype(BF16)
    for f in range(frames):
        arrive[f].wait()
        if f == 0:
            loads[0].start()

        normed[f] = layer_normed(x[f], gain[0]).astype(BF16)
        keyed[f, band] = layer_normed(dot(pool, normed[f]), gain[1]).astype(BF16)
        if f == 0:
            pl.semaphore_wait(barrier, n - 1 + pairs)
        for step in range(1, pairs):
            even_copy(f, step, band).start()
        pair_copy(f, 0, band).start()
    for load in loads[1:]:
        load.start()
    loads[0].wait()

    wide = 2 * LANES
    for f in range(frames):
        @pl.loop(0, tokens_here // wide)
        def _(i):
            rows = pl.ds(pl.multiple_of(i * wide, wide), wide)
            queries[f, rows, :] = (dot(normed[f, rows, :], sq[:, :d]) * HEAD_DIM ** (-0.5)).astype(BF16)

        for step in range(1, pairs):
            even_copy(f, step, behind(band, step)).wait_recv()
            pair_copy(f, step, behind(band, step)).start()

    first_ones, second_ones = ones_split(all_keys)
    high = lax.broadcasted_iota(jnp.int32, (LANES, all_keys), 0) >= HEAD_DIM
    right = lax.broadcasted_iota(jnp.int32, (all_keys, LANES), 1) >= HEAD_DIM

    for f in range(frames):
        for step in range(pairs):
            pair_copy(f, step, behind(partner, step)).wait_recv()
        rows = keyed[f].reshape(all_keys, d)
        for h in range(0, slabs, 2):
            both_k = dot(rows, sq[:, d + h * LANES : d + (h + 2) * LANES])
            both_v = dot(rows, sq[:, 2 * d + h * LANES : 2 * d + (h + 2) * LANES])
            for i in range(2):
                k = both_k[:, i * LANES : (i + 1) * LANES].T
                v = both_v[:, i * LANES : (i + 1) * LANES]
                kst[f, h + i] = jnp.concatenate(
                    [jnp.where(high, 0.0, k).astype(BF16), jnp.where(high, k, 0.0).astype(BF16)], axis=1
                )
                vst[f, h + i, :all_keys, :] = jnp.concatenate(
                    [jnp.where(right, 0.0, v).astype(BF16), first_ones], axis=1
                )
                vst[f, h + i, all_keys:, :] = jnp.concatenate(
                    [jnp.where(right, v, 0.0).astype(BF16), second_ones], axis=1
                )
    loads[1].wait()

    def out_copy(j, step, slot):
        return pltpu.make_async_remote_copy(
            src_ref=send1.at[j, :, lax.rem(me + step, n)], dst_ref=recv1.at[j, :, slot],
            send_sem=s1_send.at[j, step], recv_sem=s1_recv.at[j, step],
            device_id={"tm": lax.rem(me + step, n)}, device_id_type=MESH,
        )

    def back_copy(j, step, slot):
        return pltpu.make_async_remote_copy(
            src_ref=send2.at[j, :, lax.rem(me + step, n)], dst_ref=recv2.at[j, :, slot],
            send_sem=s2_send.at[j, step], recv_sem=s2_recv.at[j, step],
            device_id={"tm": lax.rem(me + step, n)}, device_id_type=MESH,
        )

    def rows_of(j, r):
        return pl.ds(pl.multiple_of(r * share + j * part, part), part)

    def spatial(j, carry):
        mixed = []
        for f in range(frames):
            q = jnp.concatenate([queries[f, rows_of(j, r), :] for r in range(n)], axis=0)
            heads = []
            for h in range(slabs):
                qh = q[:, h * LANES : (h + 1) * LANES]
                s = dot(qh, kst[f, h])
                a, b = s[:, :all_keys], s[:, all_keys:]
                a = jnp.exp(a - jnp.max(a, -1, keepdims=True)).astype(BF16)
                b = jnp.exp(b - jnp.max(b, -1, keepdims=True)).astype(BF16)
                o = dot(jnp.concatenate([a, b], axis=1), vst[f, h])
                heads.append((o[:, :LANES] / o[:, LANES:]).astype(BF16))
            mixed.append(jnp.concatenate(heads, axis=1))
        summed = dot(jnp.concatenate(mixed, axis=0), so[...])
        own = jnp.concatenate([x[f, rows_of(j, r), :] for f in range(frames) for r in range(n)], axis=0)
        first = (own.astype(F32) + summed).astype(BF16)
        fs[j] = first.reshape(frames, n, part, d)
        send1[j] = layer_normed(first, gain[2]).astype(BF16).reshape(frames, n, part, d)
        recv1[j, :, me] = send1[j, :, me]
        for step in order:
            out_copy(j, step, me).start()
        return carry

    lax.fori_loop(0, steps, spatial, 0)
    loads[2].wait()

    cells = frames * n * GROUP
    g_first, g_second = ones_split(cells)
    g_right = lax.broadcasted_iota(jnp.int32, (cells, LANES), 1) >= HEAD_DIM
    row_at = lax.broadcasted_iota(jnp.int32, (cells, cells), 0) % GROUP
    col_at = lax.broadcasted_iota(jnp.int32, (cells, cells), 1) % GROUP
    bias = jnp.where(row_at == col_at, 0.0, -1e30).astype(F32)

    def temporal(j, carry):
        for step in range(1, n):
            out_copy(j, step, lax.rem(me + n - step, n)).wait_recv()
        base = recv1[j].reshape(chunk, d)
        for c in range(3):
            part_proj = dot(base, tq[:, c * d : (c + 1) * d])
            if c == 0:
                part_proj = part_proj * HEAD_DIM ** (-0.5)
            proj[:, :, c * d : (c + 1) * d] = part_proj.astype(BF16).reshape(frames * n, part, d)
        zero = jnp.zeros((cells, LANES), BF16)
        for g in range(part // GROUP):
            at = slice(g * GROUP, (g + 1) * GROUP)
            heads = []
            for h in range(slabs):
                q, k, v = (
                    proj[:, at, c * d + h * LANES : c * d + (h + 1) * LANES].reshape(cells, LANES) for c in range(3)
                )
                kk = jnp.concatenate([jnp.where(g_right, zero, k), jnp.where(g_right, k, zero)], axis=0)
                vv = jnp.concatenate(
                    [
                        jnp.concatenate([jnp.where(g_right, zero, v), g_first], axis=1),
                        jnp.concatenate([jnp.where(g_right, v, zero), g_second], axis=1),
                    ],
                    axis=0,
                )
                s = dot_t(q, kk)
                a, b = s[:, :cells] + bias, s[:, cells:] + bias
                a = jnp.exp(a - jnp.max(a, -1, keepdims=True)).astype(BF16)
                b = jnp.exp(b - jnp.max(b, -1, keepdims=True)).astype(BF16)
                o = dot(jnp.concatenate([a, b], axis=1), vv)
                heads.append((o[:, :LANES] / o[:, LANES:]).astype(BF16))
            send2[j, :, :, at, :] = jnp.concatenate(heads, axis=1).reshape(frames, n, GROUP, d)
        recv2[j, :, me] = send2[j, :, me]
        for step in order:
            back_copy(j, step, me).start()
        return carry

    lax.fori_loop(0, steps, temporal, 0)
    for load in loads[3:]:
        load.wait()

    hidden_part = d

    def finish(j, carry):
        for step in range(1, n):
            out_copy(j, step, me).wait_send()
        for step in range(1, n):
            back_copy(j, step, lax.rem(me + n - step, n)).wait_recv()
        mix = recv2[j].reshape(chunk, d)
        second = (fs[j].reshape(chunk, d).astype(F32) + dot(mix, to[...])).astype(BF16)
        third = layer_normed(second, gain[3]).astype(BF16)
        total = second.astype(F32)
        for c in range(m1.shape[1] // hidden_part):
            span = slice(c * hidden_part, (c + 1) * hidden_part)
            u = dot(third, m1[:, span])
            u = (0.5 * u * (1.0 + lax.erf(u * 0.5**0.5))).astype(BF16)
            total = total + dot(u, m2[span, :])
        rows = pl.ds(pl.multiple_of(j * part, part), part)
        out_ref[:, :, rows, :] = total.astype(BF16).reshape(frames, n, part, d)
        return carry

    lax.fori_loop(0, steps, finish, 0)

    for f in range(frames):
        for step in range(1, pairs):
            even_copy(f, step, band).wait_send()
        for step in range(pairs):
            pair_copy(f, step, behind(band, step)).wait_send()

    def drain(j, carry):
        for step in range(1, n):
            back_copy(j, step, me).wait_send()
        return carry

    lax.fori_loop(0, steps, drain, 0)


def local(n, nb, tokens, norm_gains, spatial_qkv, spatial_out, temporal_qkv, temporal_out, mlp_in, mlp_out):
    frames, rows, cols, d = tokens.shape
    tokens_here = rows * cols
    keys = tokens_here // (POOL * POOL)
    share = tokens_here // n
    part = min(2 * GROUP, share)
    steps = share // part
    slabs = d // LANES
    all_keys = nb * keys
    far_spec = pl.BlockSpec(memory_space=pltpu.HBM)
    vmem_spec = pl.BlockSpec(memory_space=pltpu.VMEM)
    moved = pltpu.VMEM((steps, frames, n, part, d), BF16)
    dma = pltpu.SemaphoreType.DMA
    result = pl.pallas_call(
        functools.partial(block_kernel, n, nb, cols, part),
        out_shape=pltpu.VMEM((frames, n, share, d), BF16),
        in_specs=[far_spec, vmem_spec] + [far_spec] * 6,
        out_specs=vmem_spec,
        scratch_shapes=[
            pltpu.VMEM((frames, tokens_here, d), BF16),
            pltpu.VMEM(spatial_qkv.shape, BF16),
            pltpu.VMEM(spatial_out.shape, BF16),
            pltpu.VMEM(temporal_qkv.shape, BF16),
            pltpu.VMEM(temporal_out.shape, BF16),
            pltpu.VMEM(mlp_in.shape, BF16),
            pltpu.VMEM(mlp_out.shape, BF16),
            pltpu.VMEM((frames, tokens_here, d), BF16),
            pltpu.VMEM((frames, tokens_here, d), BF16),
            pltpu.VMEM((frames, nb, keys, d), BF16),
            pltpu.VMEM((frames, slabs, LANES, 2 * all_keys), BF16),
            pltpu.VMEM((frames, slabs, 2 * all_keys, 2 * LANES), BF16),
            moved, moved, moved, moved, moved,
            pltpu.VMEM((frames * n, part, 3 * d), BF16),
            dma((frames,)), dma((6,)),
            dma((frames, nb // 2)), dma((frames, nb // 2)), dma((frames, nb // 2)), dma((frames, nb // 2)),
            dma((steps, n)), dma((steps, n)), dma((steps, n)), dma((steps, n)),
        ],
        compiler_params=pltpu.CompilerParams(
            collective_id=0, has_side_effects=True, vmem_limit_bytes=54 * 1024 * 1024
        ),
        name="block",
    )(
        tokens.reshape(frames, tokens_here, d), norm_gains, spatial_qkv, spatial_out,
        temporal_qkv, temporal_out, mlp_in, mlp_out,
    )
    return result.reshape(tokens.shape)


def solution(mesh):
    n, nb = mesh.shape["tm"], mesh.shape["band"]
    in_specs = (P("tm", "band", None, None), P(), P(), P(), P(), P(), P(), P())
    out_specs = P("tm", "band", None, None)
    return jax.shard_map(
        functools.partial(local, n, nb), mesh=mesh, in_specs=in_specs, out_specs=out_specs, check_vma=False
    )
```
